256 devices in a mesh: gz: 16 (over x, y), gx: 16 (over z, core).
Axes of the slice: x: 4, y: 4, z: 8, core: 2. Of those that a mesh axis runs over, the one named last changes fastest.
Arguments:
- substrate: float32 [256, 512, 1024], P('gz', 'gx'), may hold values from 0 to 1
- catalyst: float32 [256, 512, 1024], P('gz', 'gx'), may hold values from 0 to 1
- extinction: float32 [2], replicated, may hold values from 0.25 to 1
- emission: float32 [3, 2], replicated, may hold values from 0.5 to 2
Outputs:
- substrate_next: float32 [256, 512, 1024], P('gz', 'gx')
- catalyst_next: float32 [256, 512, 1024], P('gz', 'gx')
- image: float32 [4, 512, 1024], P(None, 'gx', 'gz')
The draws below stay inside these ranges and needn't reach their ends.
All inputs are finite; a program needn't handle non-finite values.
Results may differ from the reference program's by a relative error of at most 0.00004.
Values sent between devices are 32-bit elements; how exact they have to be, the bound alone decides.
A program may use at most 64 MiB of HBM per device.

```python
import math
import jax
import jax.numpy as jnp

NY = 1024
STEPS = 2
NZ = 256
NX = 512


def shard_levels(rng, dims, shards, low, top_value):
    level, own = 1.0, jax.random.fold_in(rng, 6)
    for axis_at, shards_of in shards:
        steps = jnp.exp(jax.random.uniform(jax.random.fold_in(own, axis_at), (shards_of,), jnp.float32, low / len(shards), top_value / len(shards)))
        level = level * jnp.repeat(steps, dims[axis_at] // shards_of).reshape([-1 if axis == axis_at else 1 for axis in range(len(dims))])
    return level


def setup_inputs(seed: int = 0) -> dict:
    arg_keys = jax.random.split(jax.random.key(seed), 5)
    return {
        "substrate": jnp.clip(1.0 * jax.random.uniform(arg_keys[0], (NZ, NX, NY), jnp.float32) ** shard_levels(arg_keys[0], (NZ, NX, NY), ((0, 16), (1, 16)), -0.2, 0.2), 0.0, 1.0),
        "catalyst": jnp.clip(1.0 * jax.random.uniform(arg_keys[1], (NZ, NX, NY), jnp.float32) ** shard_levels(arg_keys[1], (NZ, NX, NY), ((0, 16), (1, 16)), -0.2, 0.2), 0.0, 1.0),
        "extinction": jnp.clip(jnp.exp(jax.random.uniform(arg_keys[2], (2,), jnp.float32, math.log(0.25), math.log(1.0))), 0.25, 1.0),
        "emission": jnp.clip(jnp.exp(jax.random.uniform(arg_keys[3], (3, 2), jnp.float32, math.log(0.5), math.log(2.0))), 0.5, 2.0),
    }


diffusion_rates = (0.16, 0.08)
feed_rate = 0.037
kill_rate = 0.06
optical_scale = 4.0


def laplace_of(fields):
    padded = jnp.pad(fields, ((0, 0), (1, 1), (1, 1), (0, 0)), mode="wrap")
    centre = padded[:, 1:-1, 1:-1]
    result = padded[:, 2:, 1:-1] + padded[:, :-2, 1:-1]
    result = result + padded[:, 1:-1, 2:] + padded[:, 1:-1, :-2]
    result = result + jnp.roll(centre, 1, axis=3) + jnp.roll(centre, -1, axis=3)
    return result - 6.0 * centre


def react(fields):
    laplace = laplace_of(fields)
    sub_old = fields[0]
    cat_old = fields[1]
    growth = sub_old * cat_old * cat_old
    sub_new = sub_old + diffusion_rates[0] * laplace[0] - growth + feed_rate * (1.0 - sub_old)
    cat_new = cat_old + diffusion_rates[1] * laplace[1] + growth - (feed_rate + kill_rate) * cat_old
    return jnp.stack([sub_new, cat_new])


def reference(substrate, catalyst, extinction, emission):
    fields = jnp.stack([substrate, catalyst])
    for step in range(STEPS):
        fields = react(fields)
    sub_final = fields[0]
    cat_final = fields[1]
    optical = (extinction[0] * sub_final + extinction[1] * cat_final) * (optical_scale / NZ)
    opacity = 1.0 - jnp.exp(-optical)
    before = jnp.cumsum(optical, axis=0) - optical
    weight = jnp.exp(-before) * opacity
    seen_sub = jnp.sum(weight * sub_final, axis=0)
    seen_cat = jnp.sum(weight * cat_final, axis=0)
    colour = emission[:, 0, None, None] * seen_sub[None] + emission[:, 1, None, None] * seen_cat[None]
    alpha_total = 1.0 - jnp.exp(-jnp.sum(optical, axis=0))
    image = jnp.concatenate([colour, alpha_total[None]], axis=0)
    return sub_final, cat_final, image
```

```python
import functools
import math

import jax
import jax.numpy as jnp
from jax import lax
from jax.experimental import pallas as pl
from jax.experimental.pallas import tpu as pltpu
from jax.sharding import PartitionSpec as P

MESH = pl.DeviceIdType.MESH
LANES = 128
TILE = 8
OFF = 8

rate_u, rate_w = (0.16, 0.08)
feed_rate = 0.037
kill_rate = 0.06
optical_scale = 4.0
LOG2E = 1.0 / math.log(2.0)


def kernel(depth, rows, cols, n_gz, n_gx, ext_hbm, u_hbm, w_hbm,
           out_u, out_w, recv,
           u0, w0, u1, w1, acc, send, ext_ref, ext_sem, load_sems, z_send, z_recv, r_send, r_recv, a_send, a_recv):
    gz = lax.axis_index("gz")
    gx = lax.axis_index("gx")
    up, down = lax.rem(gz + 1, n_gz), lax.rem(gz + n_gz - 1, n_gz)
    right, left = lax.rem(gx + 1, n_gx), lax.rem(gx + n_gx - 1, n_gx)
    tiles = rows // TILE
    half = tiles // 2
    ncol = cols // LANES
    first, last = 1, depth
    fields0, fields1 = (u0, w0), (u1, w1)

    ext_copy = pltpu.make_async_copy(ext_hbm, ext_ref, ext_sem)
    ext_copy.start()
    for f, (src, dst) in enumerate(((u_hbm, u0), (w_hbm, w0))):
        for k, z in enumerate((0, depth - 1)):
            for c in range(ncol):
                pltpu.make_async_copy(
                    src.at[pl.ds(z, 1), :, pl.ds(c * LANES, LANES)],
                    dst.at[pl.ds(z + 1, 1), c, pl.ds(OFF, rows), :],
                    load_sems.at[0, f, k]).start()
    for f, (src, dst) in enumerate(((u_hbm, u0), (w_hbm, w0))):
        for c in range(ncol):
            pltpu.make_async_copy(
                src.at[pl.ds(1, depth - 2), :, pl.ds(c * LANES, LANES)],
                dst.at[pl.ds(2, depth - 2), c, pl.ds(OFF, rows), :],
                load_sems.at[1, f, 0]).start()

    barrier = pltpu.get_barrier_semaphore()
    for k in range(1, n_gz):
        pl.semaphore_signal(barrier, inc=1, device_id={"gz": lax.rem(gz + k, n_gz)}, device_id_type=MESH)
    for nb in (left, right):
        pl.semaphore_signal(barrier, inc=1, device_id={"gx": nb}, device_id_type=MESH)
    pl.semaphore_wait(barrier, n_gz - 1 + 2)

    def wait_local(dst, sem):
        pltpu.make_async_copy(dst, dst, sem).wait()

    for f in range(2):
        for k, z in enumerate((first, last)):
            wait_local(fields0[f].at[pl.ds(z, 1), :, pl.ds(OFF, rows), :], load_sems.at[0, f, k])

    def z_copy(step, f, side, h):
        ref = (fields0, fields1)[step][f]
        r = pl.ds(OFF + h * half * TILE, half * TILE)
        return pltpu.make_async_remote_copy(
            src_ref=ref.at[last if side == 0 else first, :, r, :],
            dst_ref=ref.at[0 if side == 0 else depth + 1, :, r, :],
            send_sem=z_send.at[step, f, side, h], recv_sem=z_recv.at[step, f, side, h],
            device_id={"gz": up if side == 0 else down}, device_id_type=MESH)

    def r_copy(step, f, side):
        ref = (fields0, fields1)[step][f]
        return pltpu.make_async_remote_copy(
            src_ref=ref.at[pl.ds(1, depth), :, pl.ds(OFF + rows - 1 if side == 0 else OFF, 1), :],
            dst_ref=ref.at[pl.ds(1, depth), :, pl.ds(OFF - 1 if side == 0 else OFF + rows, 1), :],
            send_sem=r_send.at[step, f, side], recv_sem=r_recv.at[step, f, side],
            device_id={"gx": right if side == 0 else left}, device_id_type=MESH)

    for h in range(2):
        for f in range(2):
            for side in range(2):
                z_copy(0, f, side, h).start()
    for f in range(2):
        wait_local(fields0[f].at[pl.ds(2, depth - 2), :, pl.ds(OFF, rows), :], load_sems.at[1, f, 0])
    for f in range(2):
        for side in range(2):
            r_copy(0, f, side).start()

    lane = lax.broadcasted_iota(jnp.int32, (TILE, LANES), 1)
    is_first, is_last = lane == 0, lane == LANES - 1

    def around(ref, p, t):
        r0 = OFF + t * TILE

        def at(plane, c, r):
            return ref[plane, c, pl.ds(r, TILE), :]

        def turn(x, by):
            return pltpu.roll(x, by, 1)

        centre = at(p, 0, r0)
        before = turn(at(p, ncol - 1, r0), 1)
        own_down = turn(centre, LANES - 1)
        first_down = own_down
        for c in range(ncol):
            own_up = turn(centre, 1)
            if c + 1 < ncol:
                after = at(p, c + 1, r0)
                next_down = turn(after, LANES - 1)
            else:
                after, next_down = None, first_down
            total = jnp.where(is_first, before, own_up) + jnp.where(is_last, next_down, own_down)
            total = total + (at(p, c, r0 - 1) + at(p, c, r0 + 1))
            total = total + (at(p - 1, c, r0) + at(p + 1, c, r0))
            yield centre, total
            before, own_down, centre = own_up, next_down, after

    def react(fields, p, t):
        for (u, su), (w, sw) in zip(around(fields[0], p, t), around(fields[1], p, t)):
            uw = u * w
            growth = uw * w
            u_new = u * (1.0 - 6.0 * rate_u - feed_rate) + (su * rate_u + feed_rate) - growth
            w_new = w * (1.0 - 6.0 * rate_w - feed_rate - kill_rate) + sw * rate_w + growth
            yield u_new, w_new

    def step_one(p, ts):
        for t in ts:
            for c, (un, wn) in enumerate(react(fields0, p, t)):
                u1[p, c, pl.ds(OFF + t * TILE, TILE), :] = un
                w1[p, c, pl.ds(OFF + t * TILE, TILE), :] = wn

    edge_tiles = (0, tiles - 1)
    inner_tiles = tuple(range(1, tiles - 1))

    @pl.loop(2, depth)
    def _(p):
        step_one(p, inner_tiles)

    for f in range(2):
        for side in range(2):
            r_copy(0, f, side).wait_recv()

    @pl.loop(2, depth)
    def _(p):
        step_one(p, edge_tiles)

    halves = (tuple(range(half)), tuple(range(half, tiles)))
    for h in range(2):
        for f in range(2):
            for side in range(2):
                z_copy(0, f, side, h).wait_recv()
        for p in (first, last):
            step_one(p, halves[h])
        for f in range(2):
            for side in range(2):
                z_copy(1, f, side, h).start()
    for f in range(2):
        for side in range(2):
            r_copy(1, f, side).start()

    ext_copy.wait()
    k_u = ext_ref[0] * (-optical_scale / (depth * n_gz) * LOG2E)
    k_w = ext_ref[1] * (-optical_scale / (depth * n_gz) * LOG2E)

    def step_two(p, t):
        for c, (un, wn) in enumerate(react(fields1, p, t)):
            out_u[p - 1, pl.ds(t * TILE, TILE), pl.ds(c * LANES, LANES)] = un
            out_w[p - 1, pl.ds(t * TILE, TILE), pl.ds(c * LANES, LANES)] = wn
            yield c, un, wn, jnp.exp2(un * k_u + wn * k_w)

    def march(p, ts):
        for t in ts:
            for c, un, wn, e in step_two(p, t):
                r = pl.ds(t * TILE, TILE)
                seen_t = acc[2, c, r, :]
                after = seen_t * e
                weight = seen_t - after
                acc[0, c, r, :] += weight * un
                acc[1, c, r, :] += weight * wn
                acc[2, c, r, :] = after

    acc[0] = jnp.zeros(acc.shape[1:], jnp.float32)
    acc[1] = jnp.zeros(acc.shape[1:], jnp.float32)
    acc[2] = jnp.ones(acc.shape[1:], jnp.float32)

    @pl.loop(2, depth)
    def _(p):
        march(p, inner_tiles)

    for f in range(2):
        for side in range(2):
            r_copy(1, f, side).wait_recv()

    @pl.loop(2, depth)
    def _(p):
        march(p, edge_tiles)

    low_half = lane < LANES // 2

    def a_copy(h, k):
        to = lax.rem(gz + k, n_gz)
        return pltpu.make_async_remote_copy(
            src_ref=send.at[h, to], dst_ref=recv.at[h, gz],
            send_sem=a_send.at[h, k], recv_sem=a_recv.at[h, k],
            device_id={"gz": to}, device_id_type=MESH)

    for h in range(2):
        for f in range(2):
            for side in range(2):
                z_copy(1, f, side, h).wait_recv()
        march(last, halves[h])
        for t in halves[h]:
            r = pl.ds(t * TILE, TILE)
            for c, un, wn, e in step_two(first, t):
                weight = 1.0 - e
                acc[0, c, r, :] = weight * un + e * acc[0, c, r, :]
                acc[1, c, r, :] = weight * wn + e * acc[1, c, r, :]
                acc[2, c, r, :] = e * acc[2, c, r, :]
        t0, t1 = halves[h]
        for ch in range(3):
            for c in range(ncol):
                a = acc[ch, c, pl.ds(t0 * TILE, TILE), :]
                b = acc[ch, c, pl.ds(t1 * TILE, TILE), :]
                a_turned = pltpu.roll(a, LANES // 2, 1)
                b_turned = pltpu.roll(b, LANES // 2, 1)
                send[h, 2 * c, ch] = jnp.where(low_half, a, b_turned)
                send[h, 2 * c + 1, ch] = jnp.where(low_half, a_turned, b)
        for k in range(1, n_gz):
            a_copy(h, k).start()
        recv[h, gz] = send[h, gz]

    for h in range(2):
        for k in range(1, n_gz):
            a_copy(h, k).wait_recv()
    for step in range(2):
        for f in range(2):
            for side in range(2):
                for h in range(2):
                    z_copy(step, f, side, h).wait_send()
                r_copy(step, f, side).wait_send()
    for h in range(2):
        for k in range(1, n_gz):
            a_copy(h, k).wait_send()


def finish(rows, n_gz, em_hbm, u_vmem, w_vmem, recv, out_u, out_w, out_image, em_ref, image, sems):
    copies = [pltpu.make_async_copy(em_hbm, em_ref, sems.at[0]),
              pltpu.make_async_copy(u_vmem, out_u, sems.at[1]),
              pltpu.make_async_copy(w_vmem, out_w, sems.at[2])]
    for copy in copies:
        copy.start()
    copies[0].wait()
    half = rows // TILE // 2
    for h in range(2):
        zero = jnp.zeros((TILE, LANES), jnp.float32)
        seen_u, seen_w, through = zero, zero, zero + 1.0
        for k in range(n_gz):
            seen_u = seen_u + through * recv[h, k, 0]
            seen_w = seen_w + through * recv[h, k, 1]
            through = through * recv[h, k, 2]
        for ch in range(4):
            if ch < 3:
                value = em_ref[0, ch] * seen_u + em_ref[1, ch] * seen_w
            else:
                value = 1.0 - through
            for q in range(2):
                part = pltpu.roll(value, LANES // 2, 1) if q else value
                image[ch, pl.ds((h * half + q) * TILE, TILE), :] = part[:, :LANES // 2]
    copy = pltpu.make_async_copy(image, out_image, sems.at[3])
    copy.start()
    copy.wait()
    copies[1].wait()
    copies[2].wait()


def body(substrate, catalyst, extinction, emission):
    depth, rows, cols = substrate.shape
    n_gz, n_gx = lax.axis_size("gz"), lax.axis_size("gx")
    ncol = cols // LANES
    f32 = jnp.float32
    field = pltpu.VMEM((depth + 2, ncol, rows + 2 * OFF, LANES), f32)
    sds = jax.ShapeDtypeStruct
    dma = pltpu.SemaphoreType.DMA
    any_spec, vmem_spec = pl.BlockSpec(memory_space=pl.ANY), pl.BlockSpec(memory_space=pltpu.VMEM)
    shape_of = sds(substrate.shape, f32)
    substrate = pltpu.with_memory_space_constraint(substrate, pltpu.HBM)
    catalyst = pltpu.with_memory_space_constraint(catalyst, pltpu.HBM)
    extinction = pltpu.with_memory_space_constraint(extinction, pltpu.HBM)
    emission = pltpu.with_memory_space_constraint(emission.T, pltpu.HBM)
    u_new, w_new, recv = pl.pallas_call(
        functools.partial(kernel, depth, rows, cols, n_gz, n_gx),
        name="gray_scott_rays",
        out_shape=(shape_of, shape_of, sds((2, n_gz, 3, TILE, LANES), f32)),
        in_specs=[any_spec] * 3,
        out_specs=(vmem_spec,) * 3,
        scratch_shapes=[
            field, field, field, field,
            pltpu.VMEM((3, ncol, rows, LANES), f32),
            pltpu.VMEM((2, n_gz, 3, TILE, LANES), f32),
            pltpu.SMEM((2,), f32), dma(()),
            dma((2, 2, 2)), dma((2, 2, 2, 2)), dma((2, 2, 2, 2)), dma((2, 2, 2)), dma((2, 2, 2)),
            dma((2, n_gz)), dma((2, n_gz)),
        ],
        compiler_params=pltpu.CompilerParams(
            collective_id=0, has_side_effects=True, vmem_limit_bytes=40 * 2**20),
    )(extinction, substrate, catalyst)
    return tuple(pl.pallas_call(
        functools.partial(finish, rows, n_gz),
        name="write_out",
        out_shape=(shape_of, shape_of, sds((4, rows, cols // n_gz), f32)),
        in_specs=[any_spec] + [vmem_spec] * 3,
        out_specs=(any_spec,) * 3,
        scratch_shapes=[pltpu.SMEM((2, 3), f32), pltpu.VMEM((4, rows, cols // n_gz), f32), dma((4,))],
        compiler_params=pltpu.CompilerParams(vmem_limit_bytes=8 * 2**20),
    )(emission, u_new, w_new, recv))


def solution(mesh):
    placed = (P("gz", "gx", None), P("gz", "gx", None), P(), P())
    return jax.shard_map(
        body,
        mesh=mesh,
        in_specs=placed,
        out_specs=(P("gz", "gx", None), P("gz", "gx", None), P(None, "gx", "gz")),
        check_vma=False,
    )
```

```python
import functools
import math

import jax
import jax.numpy as jnp
from jax import lax
from jax.experimental import pallas as pl
from jax.experimental.pallas import tpu as pltpu
from jax.sharding import PartitionSpec as P

MESH = pl.DeviceIdType.MESH
LANES = 128
TILE = 8
OFF = 8
HALO = 2

rate_u, rate_w = (0.16, 0.08)
feed_rate = 0.037
kill_rate = 0.06
optical_scale = 4.0
LOG2E = 1.0 / math.log(2.0)


def kernel(depth, rows, cols, n_gz, n_gx, ext_hbm, u_hbm, w_hbm,
           out_u, out_w, recv,
           u0, w0, u1, w1, acc, send, row_out, row_in, corner_out, corner_in, ext_ref, ext_sem, load_sems,
           here_sems, z_send, z_recv, r_send, r_recv, c_send, c_recv, a_send, a_recv):
    gz = lax.axis_index("gz")
    gx = lax.axis_index("gx")
    tiles = rows // TILE
    ncol = cols // LANES
    first, last = HALO, HALO + depth - 1
    shells = (first - 1, last + 1)
    groups = tile_groups(tiles)
    spans_of = ((1, tiles - 2), (0, 1), (tiles - 1, 1))
    fields = ((u0, w0), (u1, w1))

    def gz_at(k):
        return {"gz": lax.rem(gz + (k + n_gz), n_gz)}

    def gx_at(k):
        return {"gx": lax.rem(gx + (k + n_gx), n_gx)}

    barrier = pltpu.get_barrier_semaphore()
    for k in (1, -1):
        pl.semaphore_signal(barrier, inc=1, device_id=gz_at(k), device_id_type=MESH)
        pl.semaphore_signal(barrier, inc=1, device_id=gx_at(k), device_id_type=MESH)

    for f, src in enumerate((u_hbm, w_hbm)):
        for k, z in enumerate((0, depth - 1)):
            for c in range(ncol):
                pltpu.make_async_copy(
                    src.at[pl.ds(z, 1), :, pl.ds(c * LANES, LANES)],
                    fields[0][f].at[pl.ds(z + HALO, 1), c, pl.ds(OFF, rows), :],
                    load_sems.at[0, f, k]).start()
    for f, src in enumerate((u_hbm, w_hbm)):
        for c in range(ncol):
            pltpu.make_async_copy(
                src.at[pl.ds(1, depth - 2), :, pl.ds(c * LANES, LANES)],
                fields[0][f].at[pl.ds(first + 1, depth - 2), c, pl.ds(OFF, rows), :],
                load_sems.at[1, f, 0]).start()
    ext_copy = pltpu.make_async_copy(ext_hbm, ext_ref, ext_sem)
    ext_copy.start()

    def wait_local(dst, sem):
        pltpu.make_async_copy(dst, dst, sem).wait()

    def z_copy(j, f, side, q):
        ref = fields[0][f]
        r = pl.ds(OFF + spans_of[q][0] * TILE, spans_of[q][1] * TILE)
        return pltpu.make_async_remote_copy(
            src_ref=ref.at[last - j if side == 0 else first + j, :, r, :],
            dst_ref=ref.at[first - 1 - j if side == 0 else last + 1 + j, :, r, :],
            send_sem=z_send.at[j, f, side, q], recv_sem=z_recv.at[j, f, side, q],
            device_id=gz_at(1 if side == 0 else -1), device_id_type=MESH)

    def corner_copy(side):
        return pltpu.make_async_remote_copy(
            src_ref=corner_out.at[side], dst_ref=corner_in.at[side],
            send_sem=c_send.at[side], recv_sem=c_recv.at[side],
            device_id=gx_at(1 if side == 0 else -1), device_id_type=MESH)

    def r_copy(step, side):
        return pltpu.make_async_remote_copy(
            src_ref=row_out.at[step, side], dst_ref=row_in.at[step, side],
            send_sem=r_send.at[step, side], recv_sem=r_recv.at[step, side],
            device_id=gx_at(1 if side == 0 else -1), device_id_type=MESH)

    def send_rows(step):
        for side in range(2):
            r = OFF + rows - 1 if side == 0 else OFF
            for f in range(2):
                for c in range(ncol):
                    row_out[step, side, f, c] = fields[step][f][pl.ds(first, depth), c, r, :]
            r_copy(step, side).start()

    def take_rows(step):
        for side in range(2):
            r = OFF - 1 if side == 0 else OFF + rows
            r_copy(step, side).wait_recv()
            for f in range(2):
                for c in range(ncol):
                    fields[step][f][pl.ds(first, depth), c, r, :] = row_in[step, side, f, c]

    def send_corners():
        for side in range(2):
            r = OFF + rows - 1 if side == 0 else OFF
            for f in range(2):
                for k in range(2):
                    corner_out[side, f, k] = fields[0][f][shells[k], pl.ds(0, ncol), r, :]
            corner_copy(side).start()

    def take_corners():
        for side in range(2):
            r = OFF - 1 if side == 0 else OFF + rows
            corner_copy(side).wait_recv()
            for f in range(2):
                for k in range(2):
                    fields[0][f][shells[k], pl.ds(0, ncol), r, :] = corner_in[side, f, k]

    def each_z(step, g, act):
        for q in ((0,), (1, 2))[g]:
            for f in range(2):
                for side in range(2):
                    act(z_copy(step, f, side, q))

    pl.semaphore_wait(barrier, 4)
    spans = []
    while (1 << len(spans)) < n_gz // 2:
        spans.append(1 << len(spans))

    def tell(i):
        if i < len(spans):
            for k in (spans[i], -spans[i]):
                pl.semaphore_signal(here_sems.at[i], inc=1, device_id=gz_at(k), device_id_type=MESH)

    def hear(i):
        if i < len(spans):
            pl.semaphore_wait(here_sems.at[i], 2)

    for f in range(2):
        for k, z in enumerate((first, last)):
            wait_local(fields[0][f].at[pl.ds(z, 1), :, pl.ds(OFF, rows), :], load_sems.at[0, f, k])
    each_z(0, 0, lambda copy: copy.start())
    tell(0)
    for f in range(2):
        wait_local(fields[0][f].at[pl.ds(first + 1, depth - 2), :, pl.ds(OFF, rows), :], load_sems.at[1, f, 0])
    send_rows(0)
    each_z(0, 1, lambda copy: copy.start())
    each_z(1, 0, lambda copy: copy.start())

    lane = lax.broadcasted_iota(jnp.int32, (TILE, LANES), 1)
    is_first, is_last = lane == 0, lane == LANES - 1

    def around(ref, p, t):
        r0 = OFF + t * TILE

        def at(plane, c, r):
            return ref[plane, c, pl.ds(r, TILE), :]

        def turn(x, by):
            return pltpu.roll(x, by, 1)

        centre = at(p, 0, r0)
        before = turn(at(p, ncol - 1, r0), 1)
        own_down = turn(centre, LANES - 1)
        first_down = own_down
        for c in range(ncol):
            own_up = turn(centre, 1)
            if c + 1 < ncol:
                after = at(p, c + 1, r0)
                next_down = turn(after, LANES - 1)
            else:
                after, next_down = None, first_down
            total = jnp.where(is_first, before, own_up) + jnp.where(is_last, next_down, own_down)
            total = total + (at(p, c, r0 - 1) + at(p, c, r0 + 1))
            total = total + (at(p - 1, c, r0) + at(p + 1, c, r0))
            yield centre, total
            before, own_down, centre = own_up, next_down, after

    def react(step, p, t):
        for (u, su), (w, sw) in zip(around(fields[step][0], p, t), around(fields[step][1], p, t)):
            uw = u * w
            growth = uw * w
            u_new = u * (1.0 - 6.0 * rate_u - feed_rate) + (su * rate_u + feed_rate) - growth
            w_new = w * (1.0 - 6.0 * rate_w - feed_rate - kill_rate) + sw * rate_w + growth
            yield u_new, w_new

    def step_one(p, ts):
        for t in ts:
            for c, (un, wn) in enumerate(react(0, p, t)):
                u1[p, c, pl.ds(OFF + t * TILE, TILE), :] = un
                w1[p, c, pl.ds(OFF + t * TILE, TILE), :] = wn

    def inside(act):
        @pl.loop(first + 1, last)
        def _(p):
            act(p)

    inner, edges = groups

    inside(lambda p: step_one(p, inner))
    hear(0)
    tell(1)
    take_rows(0)
    inside(lambda p: step_one(p, edges))
    hear(1)
    tell(2)
    for g, group in enumerate(groups):
        each_z(0, g, lambda copy: copy.wait_recv())
        for p in (first, last):
            step_one(p, group)
    send_corners()
    send_rows(1)
    each_z(1, 1, lambda copy: copy.start())

    ext_copy.wait()
    k_u = ext_ref[0] * (-optical_scale / (depth * n_gz) * LOG2E)
    k_w = ext_ref[1] * (-optical_scale / (depth * n_gz) * LOG2E)

    def step_two(p, t):
        for c, (un, wn) in enumerate(react(1, p, t)):
            out_u[p - first, pl.ds(t * TILE, TILE), pl.ds(c * LANES, LANES)] = un
            out_w[p - first, pl.ds(t * TILE, TILE), pl.ds(c * LANES, LANES)] = wn
            yield c, un, wn, jnp.exp2(un * k_u + wn * k_w)

    def march(p, ts):
        for t in ts:
            r = pl.ds(t * TILE, TILE)
            for c, un, wn, e in step_two(p, t):
                through = acc[2, c, r, :]
                after = through * e
                weight = through - after
                acc[0, c, r, :] += weight * un
                acc[1, c, r, :] += weight * wn
                acc[2, c, r, :] = after

    acc[0] = jnp.zeros(acc.shape[1:], jnp.float32)
    acc[1] = jnp.zeros(acc.shape[1:], jnp.float32)
    acc[2] = jnp.ones(acc.shape[1:], jnp.float32)

    inside(lambda p: march(p, inner))
    hear(2)

    low_half = lane < LANES // 2

    side = 4 if n_gz % 4 == 0 else 1
    turns = [(i, j) for i in range(n_gz // side) for j in range(side) if i or j]
    turns.sort(key=lambda t: -(min(t[0], n_gz // side - t[0]) + min(t[1], side - t[1])))

    def a_copy(h, i, j):
        fast = lax.rem(gz, side)
        to = lax.rem(gz - fast + i * side, n_gz) + lax.rem(fast + j, side)
        return pltpu.make_async_remote_copy(
            src_ref=send.at[h, to], dst_ref=recv.at[h, gz],
            send_sem=a_send.at[h], recv_sem=a_recv.at[h],
            device_id={"gz": to}, device_id_type=MESH)

    def a_all(h):
        rest = pl.ds(0, n_gz - 1)
        return pltpu.make_async_remote_copy(
            src_ref=send.at[h, rest], dst_ref=recv.at[h, rest],
            send_sem=a_send.at[h], recv_sem=a_recv.at[h],
            device_id=gz_at(1), device_id_type=MESH)

    for h, group in enumerate(groups):
        if h == 1:
            take_rows(1)
            inside(lambda p: march(p, edges))
            take_corners()
        each_z(1, h, lambda copy: copy.wait_recv())
        for p in shells:
            step_one(p, group)
        march(last, group)
        for t in group:
            r = pl.ds(t * TILE, TILE)
            for c, un, wn, e in step_two(first, t):
                weight = 1.0 - e
                acc[0, c, r, :] = weight * un + e * acc[0, c, r, :]
                acc[1, c, r, :] = weight * wn + e * acc[1, c, r, :]
                acc[2, c, r, :] = e * acc[2, c, r, :]
        t0, t1 = group
        for ch in range(3):
            for c in range(ncol):
                a = acc[ch, c, pl.ds(t0 * TILE, TILE), :]
                b = acc[ch, c, pl.ds(t1 * TILE, TILE), :]
                send[h, 2 * c, ch] = jnp.where(low_half, a, pltpu.roll(b, LANES // 2, 1))
                send[h, 2 * c + 1, ch] = jnp.where(low_half, pltpu.roll(a, LANES // 2, 1), b)
        for i, j in turns:
            a_copy(h, i, j).start()
        recv[h, gz] = send[h, gz]

    for step in range(2):
        for side in range(2):
            r_copy(step, side).wait_send()
            if step:
                corner_copy(side).wait_send()
        for h in range(2):
            each_z(step, h, lambda copy: copy.wait_send())
    for h in range(2):
        a_all(h).wait_send()
    for h in range(2):
        a_all(h).wait_recv()


def tile_groups(tiles):
    return tuple(range(1, tiles - 1)), (0, tiles - 1)


def finish(rows, n_gz, em_hbm, u_vmem, w_vmem, recv, out_u, out_w, out_image, em_ref, image, sems):
    copies = [pltpu.make_async_copy(em_hbm, em_ref, sems.at[0]),
              pltpu.make_async_copy(u_vmem, out_u, sems.at[1]),
              pltpu.make_async_copy(w_vmem, out_w, sems.at[2])]
    for copy in copies:
        copy.start()
    copies[0].wait()
    for h, group in enumerate(tile_groups(rows // TILE)):
        zero = jnp.zeros((TILE, LANES), jnp.float32)
        seen_u, seen_w, through = zero, zero, zero + 1.0
        for k in range(n_gz):
            seen_u = seen_u + through * recv[h, k, 0]
            seen_w = seen_w + through * recv[h, k, 1]
            through = through * recv[h, k, 2]
        for ch in range(4):
            if ch < 3:
                value = em_ref[0, ch] * seen_u + em_ref[1, ch] * seen_w
            else:
                value = 1.0 - through
            for q in range(2):
                part = pltpu.roll(value, LANES // 2, 1) if q else value
                image[ch, pl.ds(group[q] * TILE, TILE), :] = part[:, :LANES // 2]
    copy = pltpu.make_async_copy(image, out_image, sems.at[3])
    copy.start()
    copy.wait()
    copies[1].wait()
    copies[2].wait()


def body(substrate, catalyst, extinction, emission):
    depth, rows, cols = substrate.shape
    n_gz, n_gx = lax.axis_size("gz"), lax.axis_size("gx")
    ncol = cols // LANES
    f32 = jnp.float32
    field = pltpu.VMEM((depth + 2 * HALO, ncol, rows + 2 * OFF, LANES), f32)
    sds = jax.ShapeDtypeStruct
    dma = pltpu.SemaphoreType.DMA
    any_spec, vmem_spec = pl.BlockSpec(memory_space=pl.ANY), pl.BlockSpec(memory_space=pltpu.VMEM)
    shape_of = sds(substrate.shape, f32)
    substrate = pltpu.with_memory_space_constraint(substrate, pltpu.HBM)
    catalyst = pltpu.with_memory_space_constraint(catalyst, pltpu.HBM)
    extinction = pltpu.with_memory_space_constraint(extinction, pltpu.HBM)
    emission = pltpu.with_memory_space_constraint(emission.T, pltpu.HBM)
    u_new, w_new, recv = pl.pallas_call(
        functools.partial(kernel, depth, rows, cols, n_gz, n_gx),
        name="gray_scott_rays",
        out_shape=(shape_of, shape_of, sds((2, n_gz, 3, TILE, LANES), f32)),
        in_specs=[any_spec] * 3,
        out_specs=(vmem_spec,) * 3,
        scratch_shapes=[
            field, field, field, field,
            pltpu.VMEM((3, ncol, rows, LANES), f32),
            pltpu.VMEM((2, n_gz, 3, TILE, LANES), f32),
            pltpu.VMEM((2, 2, 2, ncol, depth, LANES), f32),
            pltpu.VMEM((2, 2, 2, ncol, depth, LANES), f32),
            pltpu.VMEM((2, 2, 2, ncol, LANES), f32),
            pltpu.VMEM((2, 2, 2, ncol, LANES), f32),
            pltpu.SMEM((2,), f32), dma(()), dma((2, 2, 2)), pltpu.SemaphoreType.REGULAR((3,)),
            dma((2, 2, 2, 3)), dma((2, 2, 2, 3)), dma((2, 2)), dma((2, 2)), dma((2,)), dma((2,)),
            dma((2,)), dma((2,)),
        ],
        compiler_params=pltpu.CompilerParams(
            collective_id=0, has_side_effects=True, vmem_limit_bytes=40 * 2**20),
    )(extinction, substrate, catalyst)
    return tuple(pl.pallas_call(
        functools.partial(finish, rows, n_gz),
        name="write_out",
        out_shape=(shape_of, shape_of, sds((4, rows, cols // n_gz), f32)),
        in_specs=[any_spec] + [vmem_spec] * 3,
        out_specs=(any_spec,) * 3,
        scratch_shapes=[pltpu.SMEM((2, 3), f32), pltpu.VMEM((4, rows, cols // n_gz), f32), dma((4,))],
        compiler_params=pltpu.CompilerParams(vmem_limit_bytes=8 * 2**20),
    )(emission, u_new, w_new, recv))


def solution(mesh):
    placed = (P("gz", "gx", None), P("gz", "gx", None), P(), P())
    return jax.shard_map(
        body,
        mesh=mesh,
        in_specs=placed,
        out_specs=(P("gz", "gx", None), P("gz", "gx", None), P(None, "gx", "gz")),
        check_vma=False,
    )
```

```python
import functools
import math

import jax
import jax.numpy as jnp
from jax import lax
from jax.experimental import pallas as pl
from jax.experimental.pallas import tpu as pltpu
from jax.sharding import PartitionSpec as P

MESH = pl.DeviceIdType.MESH
LANES = 128
RANK = (0, 1, 0, 1, 0, 2, 1, 0, 1, 2, 1, 0, 1, 0, 2, 1)
TILE = 8
OFF = 8
HALO = 2

rate_u, rate_w = (0.16, 0.08)
feed_rate = 0.037
kill_rate = 0.06
optical_scale = 4.0
LOG2E = 1.0 / math.log(2.0)


def kernel(depth, rows, cols, n_gz, n_gx, ext_hbm, u_hbm, w_hbm,
           out_u, out_w, recv,
           u0, w0, u1, w1, acc, send, row_out, row_in, corner_out, corner_in, ext_ref, ext_sem, load_sems,
           here_sems, z_send, z_recv, r_send, r_recv, c_send, c_recv, a_send, a_recv):
    gz = lax.axis_index("gz")
    gx = lax.axis_index("gx")
    tiles = rows // TILE
    ncol = cols // LANES
    first, last = HALO, HALO + depth - 1
    shells = (first - 1, last + 1)
    groups = tile_groups(tiles)
    spans_of = ((1, tiles - 2), (0, 1), (tiles - 1, 1))
    fields = ((u0, w0), (u1, w1))

    def gz_at(k):
        return {"gz": lax.rem(gz + (k + n_gz), n_gz)}

    def gx_at(k):
        return {"gx": lax.rem(gx + (k + n_gx), n_gx)}

    rank = RANK if len(RANK) == n_gx else range(n_gx)

    barrier = pltpu.get_barrier_semaphore()
    for k in (1, -1):
        pl.semaphore_signal(barrier, inc=1, device_id=gz_at(k), device_id_type=MESH)

    for f, src in enumerate((u_hbm, w_hbm)):
        for k, z in enumerate((0, depth - 1)):
            for c in range(ncol):
                pltpu.make_async_copy(
                    src.at[pl.ds(z, 1), :, pl.ds(c * LANES, LANES)],
                    fields[0][f].at[pl.ds(z + HALO, 1), c, pl.ds(OFF, rows), :],
                    load_sems.at[0, f, k]).start()
    for f, src in enumerate((u_hbm, w_hbm)):
        for c in range(ncol):
            pltpu.make_async_copy(
                src.at[pl.ds(1, depth - 2), :, pl.ds(c * LANES, LANES)],
                fields[0][f].at[pl.ds(first + 1, depth - 2), c, pl.ds(OFF, rows), :],
                load_sems.at[1, f, 0]).start()
    ext_copy = pltpu.make_async_copy(ext_hbm, ext_ref, ext_sem)
    ext_copy.start()

    def wait_local(dst, sem):
        pltpu.make_async_copy(dst, dst, sem).wait()

    def z_copy(j, f, side, q):
        ref = fields[0][f]
        r = pl.ds(OFF + spans_of[q][0] * TILE, spans_of[q][1] * TILE)
        return pltpu.make_async_remote_copy(
            src_ref=ref.at[last - j if side == 0 else first + j, :, r, :],
            dst_ref=ref.at[first - 1 - j if side == 0 else last + 1 + j, :, r, :],
            send_sem=z_send.at[j, f, side, q], recv_sem=z_recv.at[j, f, side, q],
            device_id=gz_at(1 if side == 0 else -1), device_id_type=MESH)

    def corner_copy(side):
        return pltpu.make_async_remote_copy(
            src_ref=corner_out.at[side], dst_ref=corner_in.at[side],
            send_sem=c_send.at[side], recv_sem=c_recv.at[side],
            device_id=gx_at(1 if side == 0 else -1), device_id_type=MESH)

    def r_copy(step, side):
        return pltpu.make_async_remote_copy(
            src_ref=row_out.at[step, side], dst_ref=row_in.at[step, side],
            send_sem=r_send.at[step, side], recv_sem=r_recv.at[step, side],
            device_id=gx_at(1 if side == 0 else -1), device_id_type=MESH)

    def send_rows(step):
        for side in range(2):
            r = OFF + rows - 1 if side == 0 else OFF
            for f in range(2):
                for c in range(ncol):
                    row_out[step, side, f, c] = fields[step][f][pl.ds(first, depth), c, r, :]
            r_copy(step, side).start()

    def take_rows(step):
        for side in range(2):
            r = OFF - 1 if side == 0 else OFF + rows
            r_copy(step, side).wait_recv()
            for f in range(2):
                for c in range(ncol):
                    fields[step][f][pl.ds(first, depth), c, r, :] = row_in[step, side, f, c]

    def send_corners():
        for side in range(2):
            r = OFF + rows - 1 if side == 0 else OFF
            for f in range(2):
                for k in range(2):
                    corner_out[side, f, k] = fields[0][f][shells[k], pl.ds(0, ncol), r, :]
            corner_copy(side).start()

    def take_corners():
        for side in range(2):
            r = OFF - 1 if side == 0 else OFF + rows
            corner_copy(side).wait_recv()
            for f in range(2):
                for k in range(2):
                    fields[0][f][shells[k], pl.ds(0, ncol), r, :] = corner_in[side, f, k]

    def each_z(step, g, act):
        for q in ((0,), (1, 2))[g]:
            for f in range(2):
                for side in range(2):
                    act(z_copy(step, f, side, q))

    lower = sum(
        (jnp.where(gx == i, 1, 0) for i in range(n_gx) for k in (1, -1) if rank[(i + k) % n_gx] < rank[i]),
        jnp.int32(0))
    pl.semaphore_wait(barrier, 2 + lower)
    for k in (1, -1):
        pl.semaphore_signal(barrier, inc=1, device_id=gx_at(k), device_id_type=MESH)
    spans = []
    while (1 << len(spans)) < n_gz // 2:
        spans.append(1 << len(spans))

    def tell(i):
        if i < len(spans):
            for k in (spans[i], -spans[i]):
                pl.semaphore_signal(here_sems.at[i], inc=1, device_id=gz_at(k), device_id_type=MESH)

    def hear(i):
        if i < len(spans):
            pl.semaphore_wait(here_sems.at[i], 2)

    for f in range(2):
        for k, z in enumerate((first, last)):
            wait_local(fields[0][f].at[pl.ds(z, 1), :, pl.ds(OFF, rows), :], load_sems.at[0, f, k])
    each_z(0, 0, lambda copy: copy.start())
    tell(0)
    for f in range(2):
        wait_local(fields[0][f].at[pl.ds(first + 1, depth - 2), :, pl.ds(OFF, rows), :], load_sems.at[1, f, 0])
    each_z(0, 1, lambda copy: copy.start())
    each_z(1, 0, lambda copy: copy.start())
    each_z(1, 1, lambda copy: copy.start())

    lane = lax.broadcasted_iota(jnp.int32, (TILE, LANES), 1)
    is_first, is_last = lane == 0, lane == LANES - 1

    def around(ref, p, t):
        r0 = OFF + t * TILE

        def at(plane, c, r):
            return ref[plane, c, pl.ds(r, TILE), :]

        def turn(x, by):
            return pltpu.roll(x, by, 1)

        centre = at(p, 0, r0)
        before = turn(at(p, ncol - 1, r0), 1)
        own_down = turn(centre, LANES - 1)
        first_down = own_down
        for c in range(ncol):
            own_up = turn(centre, 1)
            if c + 1 < ncol:
                after = at(p, c + 1, r0)
                next_down = turn(after, LANES - 1)
            else:
                after, next_down = None, first_down
            total = jnp.where(is_first, before, own_up) + jnp.where(is_last, next_down, own_down)
            total = total + (at(p, c, r0 - 1) + at(p, c, r0 + 1))
            total = total + (at(p - 1, c, r0) + at(p + 1, c, r0))
            yield centre, total
            before, own_down, centre = own_up, next_down, after

    def react(step, p, t):
        for (u, su), (w, sw) in zip(around(fields[step][0], p, t), around(fields[step][1], p, t)):
            uw = u * w
            growth = uw * w
            u_new = u * (1.0 - 6.0 * rate_u - feed_rate) + (su * rate_u + feed_rate) - growth
            w_new = w * (1.0 - 6.0 * rate_w - feed_rate - kill_rate) + sw * rate_w + growth
            yield u_new, w_new

    def step_one(p, ts):
        for t in ts:
            for c, (un, wn) in enumerate(react(0, p, t)):
                u1[p, c, pl.ds(OFF + t * TILE, TILE), :] = un
                w1[p, c, pl.ds(OFF + t * TILE, TILE), :] = wn

    def inside(act):
        @pl.loop(first + 1, last)
        def _(p):
            act(p)

    inner, edges = groups

    inside(lambda p: step_one(p, inner))

    @pl.when(lower < 2)
    def _():
        pl.semaphore_wait(barrier, 2 - lower)

    send_rows(0)
    hear(0)
    tell(1)
    each_z(0, 0, lambda copy: copy.wait_recv())
    for p in (first, last):
        step_one(p, inner)
    take_rows(0)
    inside(lambda p: step_one(p, edges))
    hear(1)
    tell(2)
    each_z(0, 1, lambda copy: copy.wait_recv())
    for p in (first, last):
        step_one(p, edges)
    send_corners()
    send_rows(1)
    ext_copy.wait()
    k_u = ext_ref[0] * (-optical_scale / (depth * n_gz) * LOG2E)
    k_w = ext_ref[1] * (-optical_scale / (depth * n_gz) * LOG2E)

    def step_two(p, t):
        for c, (un, wn) in enumerate(react(1, p, t)):
            out_u[p - first, pl.ds(t * TILE, TILE), pl.ds(c * LANES, LANES)] = un
            out_w[p - first, pl.ds(t * TILE, TILE), pl.ds(c * LANES, LANES)] = wn
            yield c, un, wn, jnp.exp2(un * k_u + wn * k_w)

    def march(p, ts):
        for t in ts:
            r = pl.ds(t * TILE, TILE)
            for c, un, wn, e in step_two(p, t):
                through = acc[2, c, r, :]
                after = through * e
                weight = through - after
                acc[0, c, r, :] += weight * un
                acc[1, c, r, :] += weight * wn
                acc[2, c, r, :] = after

    acc[0] = jnp.zeros(acc.shape[1:], jnp.float32)
    acc[1] = jnp.zeros(acc.shape[1:], jnp.float32)
    acc[2] = jnp.ones(acc.shape[1:], jnp.float32)

    inside(lambda p: march(p, inner))
    hear(2)

    low_half = lane < LANES // 2

    side = 4 if n_gz % 4 == 0 else 1
    turns = [(i, j) for i in range(n_gz // side) for j in range(side) if i or j]
    turns.sort(key=lambda t: -(min(t[0], n_gz // side - t[0]) + min(t[1], side - t[1])))

    def a_copy(h, i, j):
        fast = lax.rem(gz, side)
        to = lax.rem(gz - fast + i * side, n_gz) + lax.rem(fast + j, side)
        return pltpu.make_async_remote_copy(
            src_ref=send.at[h, to], dst_ref=recv.at[h, gz],
            send_sem=a_send.at[h], recv_sem=a_recv.at[h],
            device_id={"gz": to}, device_id_type=MESH)

    def a_all(h):
        rest = pl.ds(0, n_gz - 1)
        return pltpu.make_async_remote_copy(
            src_ref=send.at[h, rest], dst_ref=recv.at[h, rest],
            send_sem=a_send.at[h], recv_sem=a_recv.at[h],
            device_id=gz_at(1), device_id_type=MESH)

    for h, group in enumerate(groups):
        if h == 1:
            take_rows(1)
            inside(lambda p: march(p, edges))
            take_corners()
        each_z(1, h, lambda copy: copy.wait_recv())
        for p in shells:
            step_one(p, group)
        march(last, group)
        for t in group:
            r = pl.ds(t * TILE, TILE)
            for c, un, wn, e in step_two(first, t):
                weight = 1.0 - e
                acc[0, c, r, :] = weight * un + e * acc[0, c, r, :]
                acc[1, c, r, :] = weight * wn + e * acc[1, c, r, :]
                acc[2, c, r, :] = e * acc[2, c, r, :]
        t0, t1 = group
        for ch in range(3):
            for c in range(ncol):
                a = acc[ch, c, pl.ds(t0 * TILE, TILE), :]
                b = acc[ch, c, pl.ds(t1 * TILE, TILE), :]
                send[h, 2 * c, ch] = jnp.where(low_half, a, pltpu.roll(b, LANES // 2, 1))
                send[h, 2 * c + 1, ch] = jnp.where(low_half, pltpu.roll(a, LANES // 2, 1), b)
        for i, j in turns:
            a_copy(h, i, j).start()
        recv[h, gz] = send[h, gz]

    for step in range(2):
        for side in range(2):
            r_copy(step, side).wait_send()
            if step:
                corner_copy(side).wait_send()
        for h in range(2):
            each_z(step, h, lambda copy: copy.wait_send())
    for h in range(2):
        a_all(h).wait_send()
    for h in range(2):
        a_all(h).wait_recv()


def tile_groups(tiles):
    return tuple(range(1, tiles - 1)), (0, tiles - 1)


def finish(rows, n_gz, em_hbm, u_vmem, w_vmem, recv, out_u, out_w, out_image, em_ref, image, sems):
    copies = [pltpu.make_async_copy(em_hbm, em_ref, sems.at[0]),
              pltpu.make_async_copy(u_vmem, out_u, sems.at[1]),
              pltpu.make_async_copy(w_vmem, out_w, sems.at[2])]
    for copy in copies:
        copy.start()
    copies[0].wait()
    for h, group in enumerate(tile_groups(rows // TILE)):
        zero = jnp.zeros((TILE, LANES), jnp.float32)
        seen_u, seen_w, through = zero, zero, zero + 1.0
        for k in range(n_gz):
            seen_u = seen_u + through * recv[h, k, 0]
            seen_w = seen_w + through * recv[h, k, 1]
            through = through * recv[h, k, 2]
        for ch in range(4):
            if ch < 3:
                value = em_ref[0, ch] * seen_u + em_ref[1, ch] * seen_w
            else:
                value = 1.0 - through
            for q in range(2):
                part = pltpu.roll(value, LANES // 2, 1) if q else value
                image[ch, pl.ds(group[q] * TILE, TILE), :] = part[:, :LANES // 2]
    copy = pltpu.make_async_copy(image, out_image, sems.at[3])
    copy.start()
    copy.wait()
    copies[1].wait()
    copies[2].wait()


def body(substrate, catalyst, extinction, emission):
    depth, rows, cols = substrate.shape
    n_gz, n_gx = lax.axis_size("gz"), lax.axis_size("gx")
    ncol = cols // LANES
    f32 = jnp.float32
    field = pltpu.VMEM((depth + 2 * HALO, ncol, rows + 2 * OFF, LANES), f32)
    sds = jax.ShapeDtypeStruct
    dma = pltpu.SemaphoreType.DMA
    any_spec, vmem_spec = pl.BlockSpec(memory_space=pl.ANY), pl.BlockSpec(memory_space=pltpu.VMEM)
    shape_of = sds(substrate.shape, f32)
    substrate = pltpu.with_memory_space_constraint(substrate, pltpu.HBM)
    catalyst = pltpu.with_memory_space_constraint(catalyst, pltpu.HBM)
    extinction = pltpu.with_memory_space_constraint(extinction, pltpu.HBM)
    emission = pltpu.with_memory_space_constraint(emission.T, pltpu.HBM)
    u_new, w_new, recv = pl.pallas_call(
        functools.partial(kernel, depth, rows, cols, n_gz, n_gx),
        name="gray_scott_rays",
        out_shape=(shape_of, shape_of, sds((2, n_gz, 3, TILE, LANES), f32)),
        in_specs=[any_spec] * 3,
        out_specs=(vmem_spec,) * 3,
        scratch_shapes=[
            field, field, field, field,
            pltpu.VMEM((3, ncol, rows, LANES), f32),
            pltpu.VMEM((2, n_gz, 3, TILE, LANES), f32),
            pltpu.VMEM((2, 2, 2, ncol, depth, LANES), f32),
            pltpu.VMEM((2, 2, 2, ncol, depth, LANES), f32),
            pltpu.VMEM((2, 2, 2, ncol, LANES), f32),
            pltpu.VMEM((2, 2, 2, ncol, LANES), f32),
            pltpu.SMEM((2,), f32), dma(()), dma((2, 2, 2)), pltpu.SemaphoreType.REGULAR((3,)),
            dma((2, 2, 2, 3)), dma((2, 2, 2, 3)), dma((2, 2)), dma((2, 2)), dma((2,)), dma((2,)),
            dma((2,)), dma((2,)),
        ],
        compiler_params=pltpu.CompilerParams(
            collective_id=0, has_side_effects=True, vmem_limit_bytes=40 * 2**20),
    )(extinction, substrate, catalyst)
    return tuple(pl.pallas_call(
        functools.partial(finish, rows, n_gz),
        name="write_out",
        out_shape=(shape_of, shape_of, sds((4, rows, cols // n_gz), f32)),
        in_specs=[any_spec] + [vmem_spec] * 3,
        out_specs=(any_spec,) * 3,
        scratch_shapes=[pltpu.SMEM((2, 3), f32), pltpu.VMEM((4, rows, cols // n_gz), f32), dma((4,))],
        compiler_params=pltpu.CompilerParams(vmem_limit_bytes=8 * 2**20),
    )(emission, u_new, w_new, recv))


def solution(mesh):
    placed = (P("gz", "gx", None), P("gz", "gx", None), P(), P())
    return jax.shard_map(
        body,
        mesh=mesh,
        in_specs=placed,
        out_specs=(P("gz", "gx", None), P("gz", "gx", None), P(None, "gx", "gz")),
        check_vma=False,
    )
```

```python
import functools
import math

import jax
import jax.numpy as jnp
from jax import lax
from jax.experimental import pallas as pl
from jax.experimental.pallas import tpu as pltpu
from jax.sharding import PartitionSpec as P

MESH = pl.DeviceIdType.MESH
LANES = 128
RANK = (0, 1, 0, 1, 0, 2, 1, 0, 1, 2, 1, 0, 1, 0, 2, 1)
TILE = 8
OFF = 8
HALO = 2

rate_u, rate_w = (0.16, 0.08)
feed_rate = 0.037
kill_rate = 0.06
optical_scale = 4.0
LOG2E = 1.0 / math.log(2.0)


def kernel(depth, rows, cols, n_gz, n_gx, ext_hbm, u_hbm, w_hbm,
           out_u, out_w, recv,
           u0, w0, u1, w1, acc, send, row_out, row_in, corner_out, corner_in, ext_ref, ext_sem, load_sems,
           here_sems, z_send, z_recv, r_send, r_recv, c_send, c_recv, a_send, a_recv):
    gz = lax.axis_index("gz")
    gx = lax.axis_index("gx")
    tiles = rows // TILE
    ncol = cols // LANES
    first, last = HALO, HALO + depth - 1
    shells = (first - 1, last + 1)
    groups = tile_groups(tiles)
    spans_of = ((1, tiles - 2), (0, 1), (tiles - 1, 1))
    fields = ((u0, w0), (u1, w1))

    def gz_at(k):
        return {"gz": lax.rem(gz + (k + n_gz), n_gz)}

    def gx_at(k):
        return {"gx": lax.rem(gx + (k + n_gx), n_gx)}

    rank = RANK if len(RANK) == n_gx else range(n_gx)

    barrier = pltpu.get_barrier_semaphore()
    for k in (1, -1):
        pl.semaphore_signal(barrier, inc=1, device_id=gz_at(k), device_id_type=MESH)

    for f, src in enumerate((u_hbm, w_hbm)):
        for k, z in enumerate((0, depth - 1)):
            for c in range(ncol):
                pltpu.make_async_copy(
                    src.at[pl.ds(z, 1), :, pl.ds(c * LANES, LANES)],
                    fields[0][f].at[pl.ds(z + HALO, 1), c, pl.ds(OFF, rows), :],
                    load_sems.at[0, f, k]).start()
    for f, src in enumerate((u_hbm, w_hbm)):
        for c in range(ncol):
            pltpu.make_async_copy(
                src.at[pl.ds(1, depth - 2), :, pl.ds(c * LANES, LANES)],
                fields[0][f].at[pl.ds(first + 1, depth - 2), c, pl.ds(OFF, rows), :],
                load_sems.at[1, f, 0]).start()
    ext_copy = pltpu.make_async_copy(ext_hbm, ext_ref, ext_sem)
    ext_copy.start()

    def wait_local(dst, sem):
        pltpu.make_async_copy(dst, dst, sem).wait()

    def z_copy(j, f, side, q):
        ref = fields[0][f]
        r = pl.ds(OFF + spans_of[q][0] * TILE, spans_of[q][1] * TILE)
        return pltpu.make_async_remote_copy(
            src_ref=ref.at[last - j if side == 0 else first + j, :, r, :],
            dst_ref=ref.at[first - 1 - j if side == 0 else last + 1 + j, :, r, :],
            send_sem=z_send.at[j, f, side, q], recv_sem=z_recv.at[j, f, side, q],
            device_id=gz_at(1 if side == 0 else -1), device_id_type=MESH)

    def corner_copy(side):
        return pltpu.make_async_remote_copy(
            src_ref=corner_out.at[side], dst_ref=corner_in.at[side],
            send_sem=c_send.at[side], recv_sem=c_recv.at[side],
            device_id=gx_at(1 if side == 0 else -1), device_id_type=MESH)

    def r_copy(step, side):
        return pltpu.make_async_remote_copy(
            src_ref=row_out.at[step, side], dst_ref=row_in.at[step, side],
            send_sem=r_send.at[step, side], recv_sem=r_recv.at[step, side],
            device_id=gx_at(1 if side == 0 else -1), device_id_type=MESH)

    def send_rows(step):
        for side in range(2):
            r = OFF + rows - 1 if side == 0 else OFF
            for f in range(2):
                for c in range(ncol):
                    row_out[step, side, f, c] = fields[step][f][pl.ds(first, depth), c, r, :]
            r_copy(step, side).start()

    def take_rows(step):
        for side in range(2):
            r = OFF - 1 if side == 0 else OFF + rows
            r_copy(step, side).wait_recv()
            for f in range(2):
                for c in range(ncol):
                    fields[step][f][pl.ds(first, depth), c, r, :] = row_in[step, side, f, c]

    def send_corners():
        for side in range(2):
            r = OFF + rows - 1 if side == 0 else OFF
            for f in range(2):
                for k in range(2):
                    corner_out[side, f, k] = fields[0][f][shells[k], pl.ds(0, ncol), r, :]
            corner_copy(side).start()

    def take_corners():
        for side in range(2):
            r = OFF - 1 if side == 0 else OFF + rows
            corner_copy(side).wait_recv()
            for f in range(2):
                for k in range(2):
                    fields[0][f][shells[k], pl.ds(0, ncol), r, :] = corner_in[side, f, k]

    def each_z(step, g, act):
        for q in ((0,), (1, 2))[g]:
            for f in range(2):
                for side in range(2):
                    act(z_copy(step, f, side, q))

    lower = sum(
        (jnp.where(gx == i, 1, 0) for i in range(n_gx) for k in (1, -1) if rank[(i + k) % n_gx] < rank[i]),
        jnp.int32(0))
    pl.semaphore_wait(barrier, 2 + lower)
    for k in (1, -1):
        pl.semaphore_signal(barrier, inc=1, device_id=gx_at(k), device_id_type=MESH)
    spans = []
    while (1 << len(spans)) < n_gz // 2:
        spans.append(1 << len(spans))

    def tell(i):
        if i < len(spans):
            for k in (spans[i], -spans[i]):
                pl.semaphore_signal(here_sems.at[i], inc=1, device_id=gz_at(k), device_id_type=MESH)

    def hear(i):
        if i < len(spans):
            pl.semaphore_wait(here_sems.at[i], 2)

    for f in range(2):
        for k, z in enumerate((first, last)):
            wait_local(fields[0][f].at[pl.ds(z, 1), :, pl.ds(OFF, rows), :], load_sems.at[0, f, k])
    each_z(0, 0, lambda copy: copy.start())
    tell(0)
    for f in range(2):
        wait_local(fields[0][f].at[pl.ds(first + 1, depth - 2), :, pl.ds(OFF, rows), :], load_sems.at[1, f, 0])
    each_z(0, 1, lambda copy: copy.start())
    each_z(1, 0, lambda copy: copy.start())
    each_z(1, 1, lambda copy: copy.start())

    lane = lax.broadcasted_iota(jnp.int32, (TILE, LANES), 1)
    is_first, is_last = lane == 0, lane == LANES - 1

    def around(ref, p, t):
        r0 = OFF + t * TILE

        def at(plane, c, r):
            return ref[plane, c, pl.ds(r, TILE), :]

        def turn(x, by):
            return pltpu.roll(x, by, 1)

        centre = at(p, 0, r0)
        before = turn(at(p, ncol - 1, r0), 1)
        own_down = turn(centre, LANES - 1)
        first_down = own_down
        for c in range(ncol):
            own_up = turn(centre, 1)
            if c + 1 < ncol:
                after = at(p, c + 1, r0)
                next_down = turn(after, LANES - 1)
            else:
                after, next_down = None, first_down
            total = jnp.where(is_first, before, own_up) + jnp.where(is_last, next_down, own_down)
            total = total + (at(p, c, r0 - 1) + at(p, c, r0 + 1))
            total = total + (at(p - 1, c, r0) + at(p + 1, c, r0))
            yield centre, total
            before, own_down, centre = own_up, next_down, after

    def react(step, p, t):
        for (u, su), (w, sw) in zip(around(fields[step][0], p, t), around(fields[step][1], p, t)):
            uw = u * w
            growth = uw * w
            u_new = u * (1.0 - 6.0 * rate_u - feed_rate) + (su * rate_u + feed_rate) - growth
            w_new = w * (1.0 - 6.0 * rate_w - feed_rate - kill_rate) + sw * rate_w + growth
            yield u_new, w_new

    def step_one(p, ts):
        for t in ts:
            for c, (un, wn) in enumerate(react(0, p, t)):
                u1[p, c, pl.ds(OFF + t * TILE, TILE), :] = un
                w1[p, c, pl.ds(OFF + t * TILE, TILE), :] = wn

    def inside(act):
        @pl.loop(first + 1, last, unroll=2)
        def _(p):
            act(p)

    inner, edges = groups

    inside(lambda p: step_one(p, inner))

    @pl.when(lower < 2)
    def _():
        pl.semaphore_wait(barrier, 2 - lower)

    send_rows(0)
    hear(0)
    tell(1)
    each_z(0, 0, lambda copy: copy.wait_recv())
    for p in (first, last):
        step_one(p, inner)
    take_rows(0)
    inside(lambda p: step_one(p, edges))
    hear(1)
    tell(2)
    each_z(0, 1, lambda copy: copy.wait_recv())
    for p in (first, last):
        step_one(p, edges)
    send_corners()
    send_rows(1)
    ext_copy.wait()
    k_u = ext_ref[0] * (-optical_scale / (depth * n_gz) * LOG2E)
    k_w = ext_ref[1] * (-optical_scale / (depth * n_gz) * LOG2E)

    def step_two(p, t):
        for c, (un, wn) in enumerate(react(1, p, t)):
            out_u[p - first, pl.ds(t * TILE, TILE), pl.ds(c * LANES, LANES)] = un
            out_w[p - first, pl.ds(t * TILE, TILE), pl.ds(c * LANES, LANES)] = wn
            yield c, un, wn, jnp.exp2(un * k_u + wn * k_w)

    def march(p, ts):
        for t in ts:
            r = pl.ds(t * TILE, TILE)
            for c, un, wn, e in step_two(p, t):
                through = acc[2, c, r, :]
                after = through * e
                weight = through - after
                acc[0, c, r, :] += weight * un
                acc[1, c, r, :] += weight * wn
                acc[2, c, r, :] = after

    acc[0] = jnp.zeros(acc.shape[1:], jnp.float32)
    acc[1] = jnp.zeros(acc.shape[1:], jnp.float32)
    acc[2] = jnp.ones(acc.shape[1:], jnp.float32)

    inside(lambda p: march(p, inner))
    hear(2)

    low_half = lane < LANES // 2

    side = 4 if n_gz % 4 == 0 else 1
    turns = [(i, j) for i in range(n_gz // side) for j in range(side) if i or j]
    turns.sort(key=lambda t: -(min(t[0], n_gz // side - t[0]) + min(t[1], side - t[1])))

    def a_copy(h, i, j):
        fast = lax.rem(gz, side)
        to = lax.rem(gz - fast + i * side, n_gz) + lax.rem(fast + j, side)
        return pltpu.make_async_remote_copy(
            src_ref=send.at[h, to], dst_ref=recv.at[h, gz],
            send_sem=a_send.at[h], recv_sem=a_recv.at[h],
            device_id={"gz": to}, device_id_type=MESH)

    def a_all(h):
        rest = pl.ds(0, n_gz - 1)
        return pltpu.make_async_remote_copy(
            src_ref=send.at[h, rest], dst_ref=recv.at[h, rest],
            send_sem=a_send.at[h], recv_sem=a_recv.at[h],
            device_id=gz_at(1), device_id_type=MESH)

    for h, group in enumerate(groups):
        if h == 1:
            take_rows(1)
            inside(lambda p: march(p, edges))
            take_corners()
        each_z(1, h, lambda copy: copy.wait_recv())
        for p in shells:
            step_one(p, group)
        march(last, group)
        for t in group:
            r = pl.ds(t * TILE, TILE)
            for c, un, wn, e in step_two(first, t):
                weight = 1.0 - e
                acc[0, c, r, :] = weight * un + e * acc[0, c, r, :]
                acc[1, c, r, :] = weight * wn + e * acc[1, c, r, :]
                acc[2, c, r, :] = e * acc[2, c, r, :]
        t0, t1 = group
        for ch in range(3):
            for c in range(ncol):
                a = acc[ch, c, pl.ds(t0 * TILE, TILE), :]
                b = acc[ch, c, pl.ds(t1 * TILE, TILE), :]
                send[h, 2 * c, ch] = jnp.where(low_half, a, pltpu.roll(b, LANES // 2, 1))
                send[h, 2 * c + 1, ch] = jnp.where(low_half, pltpu.roll(a, LANES // 2, 1), b)
        for i, j in turns:
            a_copy(h, i, j).start()
        recv[h, gz] = send[h, gz]

    for step in range(2):
        for side in range(2):
            r_copy(step, side).wait_send()
            if step:
                corner_copy(side).wait_send()
        for h in range(2):
            each_z(step, h, lambda copy: copy.wait_send())
    for h in range(2):
        a_all(h).wait_send()
    for h in range(2):
        a_all(h).wait_recv()


def tile_groups(tiles):
    return tuple(range(1, tiles - 1)), (0, tiles - 1)


def finish(rows, n_gz, em_hbm, u_vmem, w_vmem, recv, out_u, out_w, out_image, em_ref, image, sems):
    copies = [pltpu.make_async_copy(em_hbm, em_ref, sems.at[0]),
              pltpu.make_async_copy(u_vmem, out_u, sems.at[1]),
              pltpu.make_async_copy(w_vmem, out_w, sems.at[2])]
    for copy in copies:
        copy.start()
    copies[0].wait()
    for h, group in enumerate(tile_groups(rows // TILE)):
        zero = jnp.zeros((TILE, LANES), jnp.float32)
        seen_u, seen_w, through = zero, zero, zero + 1.0
        for k in range(n_gz):
            seen_u = seen_u + through * recv[h, k, 0]
            seen_w = seen_w + through * recv[h, k, 1]
            through = through * recv[h, k, 2]
        for ch in range(4):
            if ch < 3:
                value = em_ref[0, ch] * seen_u + em_ref[1, ch] * seen_w
            else:
                value = 1.0 - through
            for q in range(2):
                part = pltpu.roll(value, LANES // 2, 1) if q else value
                image[ch, pl.ds(group[q] * TILE, TILE), :] = part[:, :LANES // 2]
    copy = pltpu.make_async_copy(image, out_image, sems.at[3])
    copy.start()
    copy.wait()
    copies[1].wait()
    copies[2].wait()


def body(substrate, catalyst, extinction, emission):
    depth, rows, cols = substrate.shape
    n_gz, n_gx = lax.axis_size("gz"), lax.axis_size("gx")
    ncol = cols // LANES
    f32 = jnp.float32
    field = pltpu.VMEM((depth + 2 * HALO, ncol, rows + 2 * OFF, LANES), f32)
    sds = jax.ShapeDtypeStruct
    dma = pltpu.SemaphoreType.DMA
    any_spec, vmem_spec = pl.BlockSpec(memory_space=pl.ANY), pl.BlockSpec(memory_space=pltpu.VMEM)
    shape_of = sds(substrate.shape, f32)
    substrate = pltpu.with_memory_space_constraint(substrate, pltpu.HBM)
    catalyst = pltpu.with_memory_space_constraint(catalyst, pltpu.HBM)
    extinction = pltpu.with_memory_space_constraint(extinction, pltpu.HBM)
    emission = pltpu.with_memory_space_constraint(emission.T, pltpu.HBM)
    u_new, w_new, recv = pl.pallas_call(
        functools.partial(kernel, depth, rows, cols, n_gz, n_gx),
        name="gray_scott_rays",
        out_shape=(shape_of, shape_of, sds((2, n_gz, 3, TILE, LANES), f32)),
        in_specs=[any_spec] * 3,
        out_specs=(vmem_spec,) * 3,
        scratch_shapes=[
            field, field, field, field,
            pltpu.VMEM((3, ncol, rows, LANES), f32),
            pltpu.VMEM((2, n_gz, 3, TILE, LANES), f32),
            pltpu.VMEM((2, 2, 2, ncol, depth, LANES), f32),
            pltpu.VMEM((2, 2, 2, ncol, depth, LANES), f32),
            pltpu.VMEM((2, 2, 2, ncol, LANES), f32),
            pltpu.VMEM((2, 2, 2, ncol, LANES), f32),
            pltpu.SMEM((2,), f32), dma(()), dma((2, 2, 2)), pltpu.SemaphoreType.REGULAR((3,)),
            dma((2, 2, 2, 3)), dma((2, 2, 2, 3)), dma((2, 2)), dma((2, 2)), dma((2,)), dma((2,)),
            dma((2,)), dma((2,)),
        ],
        compiler_params=pltpu.CompilerParams(
            collective_id=0, has_side_effects=True, vmem_limit_bytes=40 * 2**20),
    )(extinction, substrate, catalyst)
    return tuple(pl.pallas_call(
        functools.partial(finish, rows, n_gz),
        name="write_out",
        out_shape=(shape_of, shape_of, sds((4, rows, cols // n_gz), f32)),
        in_specs=[any_spec] + [vmem_spec] * 3,
        out_specs=(any_spec,) * 3,
        scratch_shapes=[pltpu.SMEM((2, 3), f32), pltpu.VMEM((4, rows, cols // n_gz), f32), dma((4,))],
        compiler_params=pltpu.CompilerParams(vmem_limit_bytes=8 * 2**20),
    )(emission, u_new, w_new, recv))


def solution(mesh):
    placed = (P("gz", "gx", None), P("gz", "gx", None), P(), P())
    return jax.shard_map(
        body,
        mesh=mesh,
        in_specs=placed,
        out_specs=(P("gz", "gx", None), P("gz", "gx", None), P(None, "gx", "gz")),
        check_vma=False,
    )
```
